32 devices in a mesh: seq: 16 (over z, x, core), head: 2 (over y).
Axes of the slice: x: 2, y: 2, z: 4, core: 2. Of those that a mesh axis runs over, the one named last changes fastest.
Arguments:
- query: bfloat16 [2048, 8192], P(('seq', 'head')), may hold values from -6 to 6
- key: bfloat16 [2048, 8192], P(('seq', 'head')), may hold values from -6 to 6
- value: bfloat16 [2048, 8192], P(('seq', 'head')), may hold values from -6 to 6
- cotangent: bfloat16 [2048, 8192], P(('seq', 'head')), may hold values from -6 to 6
- gain: float32 [8192], P('head'), may hold values from 0.5 to 1.5
- incoming_state: float32 [64, 128, 128], P('head'), may hold values from -288 to 288
Outputs:
- output: bfloat16 [2048, 8192], P(('seq', 'head'))
- grad_query: bfloat16 [2048, 8192], P(('seq', 'head'))
- grad_key: bfloat16 [2048, 8192], P(('seq', 'head'))
- grad_value: bfloat16 [2048, 8192], P(('seq', 'head'))
The draws below stay inside these ranges and needn't reach their ends.
All inputs are finite; a program needn't handle non-finite values.
Results may differ from the reference program's by a relative error of at most 0.0058.
Values may be sent and summed in bfloat16 or wider, within the bound.
A program may use at most 128 MiB of HBM per device.

```python
import jax
import jax.numpy as jnp
from jax import lax

HEADS = 64
HEAD_DIM = 128
TOK_DEV = 128
WIDTH = 8192
TOKENS = 2048
N_SEQ = 16


def block_scale(own_key, dims, cuts, smallest, high):
    level = 1.0
    for axis_at, shards_of in cuts:
        heights = jax.random.uniform(jax.random.fold_in(jax.random.fold_in(own_key, 6), axis_at), (shards_of,), jnp.float32, smallest / len(cuts), high / len(cuts))
        level = level * jnp.repeat(jnp.exp(heights), dims[axis_at] // shards_of).reshape((-1,) + (1,) * (len(dims) - 1 - axis_at))
    return level


def centred(own_key, dims, width, limit, split=(), kind=jnp.bfloat16):
    result = jax.random.normal(own_key, dims, jnp.float32) * width
    if len(split) > 0:
        result = block_scale(own_key, dims, split, -0.22, 0.18) * result
    return jnp.clip(result, min=-limit, max=limit).astype(kind)


def setup_inputs(seed: int = 0) -> dict:
    splits = jax.random.split(jax.random.key(seed), 7)
    return {
        "query": centred(splits[0], (TOKENS, WIDTH), 1.0, 6.0, ((0, 32),)),
        "key": centred(splits[1], (TOKENS, WIDTH), 1.0, 6.0, ((0, 32),)),
        "value": centred(splits[2], (TOKENS, WIDTH), 1.0, 6.0, ((0, 32),)),
        "cotangent": centred(splits[3], (TOKENS, WIDTH), 1.0, 6.0, ((0, 32),)),
        "gain": jnp.clip(1.0 + 0.1 * jax.random.normal(splits[4], (WIDTH,), jnp.float32), 0.5, 1.5),
        "incoming_state": centred(splits[5], (HEADS, HEAD_DIM, HEAD_DIM), 48.0, 288.0, ((0, 2),), jnp.float32),
    }


EPSILON = 1e-06

def head_pass(packed):
    query_block, key_block, value_block, upstream, gain_row, carried = packed
    causal = jnp.tril(jnp.ones((TOK_DEV, TOK_DEV), dtype=bool))
    query_wide = query_block.astype(jnp.float32)
    key_wide = key_block.astype(jnp.float32)
    value_wide = value_block.astype(jnp.float32)
    scores = jnp.einsum('ctd,csd->cts', query_wide, key_wide)
    weights = jnp.where(causal, scores, 0.0).astype(jnp.bfloat16)
    weights_wide = weights.astype(jnp.float32)
    within = jnp.einsum('cts,cse->cte', weights_wide, value_wide)
    block_state = jnp.einsum('csd,cse->cde', key_wide, value_wide)
    prefix = jnp.cumsum(block_state, axis=0) - block_state + carried[None]
    states = prefix.astype(jnp.bfloat16).astype(jnp.float32)
    attention = within + jnp.einsum('ctd,cde->cte', query_wide, states)
    root_mean = jnp.sqrt(lax.optimization_barrier(jnp.mean(attention * attention, axis=-1, keepdims=True)) + EPSILON)
    normed = attention / root_mean
    output = (normed * gain_row).astype(jnp.bfloat16)
    scaled = upstream.astype(jnp.float32) * gain_row
    grad_attn = ((scaled - normed * lax.optimization_barrier(jnp.mean(scaled * normed, axis=-1, keepdims=True))) / root_mean).astype(jnp.bfloat16)
    grad_wide = grad_attn.astype(jnp.float32)
    grad_scores = jnp.where(causal, jnp.einsum('cte,cse->cts', grad_wide, value_wide), 0.0).astype(jnp.bfloat16)
    grad_scores_wide = grad_scores.astype(jnp.float32)
    grad_state = jnp.einsum('ctd,cte->cde', query_wide, grad_wide)
    suffix = jnp.cumsum(grad_state[::-1], axis=0)[::-1] - grad_state
    later_states = suffix.astype(jnp.bfloat16).astype(jnp.float32)
    grad_query = jnp.einsum('cts,csd->ctd', grad_scores_wide, key_wide) + jnp.einsum('cte,cde->ctd', grad_wide, states)
    grad_key = jnp.einsum('cts,ctd->csd', grad_scores_wide, query_wide) + jnp.einsum('cse,cde->csd', value_wide, later_states)
    grad_value = jnp.einsum('cts,cte->cse', weights_wide, grad_wide) + jnp.einsum('csd,cde->cse', key_wide, later_states)
    return (output, grad_query.astype(jnp.bfloat16), grad_key.astype(jnp.bfloat16), grad_value.astype(jnp.bfloat16))

def split_heads(array):
    return array.reshape(N_SEQ, TOK_DEV, HEADS, HEAD_DIM).transpose(2, 0, 1, 3)

def join_heads(array):
    return array.transpose(1, 2, 0, 3).reshape(TOKENS, HEADS * HEAD_DIM)

def reference(query, key, value, cotangent, gain, incoming_state):
    packed = (split_heads(query), split_heads(key), split_heads(value), split_heads(cotangent), gain.reshape(HEADS, 1, 1, HEAD_DIM), incoming_state)
    results = lax.map(head_pass, packed)
    return (join_heads(results[0]), join_heads(results[1]), join_heads(results[2]), join_heads(results[3]))
```

```python
import functools

import jax
import jax.numpy as jnp
from jax import lax
from jax.experimental import pallas as pl
from jax.experimental.pallas import tpu as pltpu
from jax.sharding import PartitionSpec as P

HEAD_DIM = 128
EPSILON = 1e-06
MESH = pl.DeviceIdType.MESH
F32 = jnp.float32
BF16 = jnp.bfloat16

NT = (((1,), (1,)), ((), ()))
TN = (((0,), (0,)), ((), ()))
NN = (((1,), (0,)), ((), ()))


def dot(a, b, dims):
    return lax.dot_general(a, b, dims, preferred_element_type=F32)


def kernel(plan, q_hbm, k_hbm, v_hbm, y_hbm, gain_hbm, s0_hbm, o_hbm, gq_hbm, gk_hbm, gv_hbm,
           xin, xout, part, cum, gcum, pin, psend, sin, ssend, tot, gain,
           in_send, in_recv, out_send, out_recv, p_send, p_recv, s_send, s_recv, gain_sem):
    n_groups, sub, n_head, rows, heads, step = plan
    peers = sub * n_head
    chunks = heads // step
    block = rows * n_head
    width = heads * HEAD_DIM
    span = step * HEAD_DIM
    seq, hd = lax.axis_index("seq"), lax.axis_index("head")
    group, j = seq // sub, lax.rem(seq, sub)
    me = j * n_head + hd

    def place(p):
        other = lax.rem(me + p, peers)
        return other, (group * sub + other // n_head, lax.rem(other, n_head))

    def column(other, c):
        owner = lax.rem(other, n_head) * (sub * heads) + (other // n_head) * heads + c * step
        return pl.ds(pl.multiple_of(owner * HEAD_DIM, span), span)

    def strip(index):
        return pl.ds(pl.multiple_of(index * rows, rows), rows)

    later = (seq + sub, hd)
    earlier = (seq - sub, hd)
    barrier = pltpu.get_barrier_semaphore()

    def greet(p, carry):
        _, device = place(p)
        pl.semaphore_signal(barrier, inc=1, device_id=device, device_id_type=MESH)
        return carry

    lax.fori_loop(1, peers, greet, 0)

    @pl.when(group > 0)
    def _():
        pl.semaphore_signal(barrier, inc=1, device_id=earlier, device_id_type=MESH)

    @pl.when(group < n_groups - 1)
    def _():
        pl.semaphore_signal(barrier, inc=1, device_id=later, device_id_type=MESH)

    sources = ((k_hbm, v_hbm), (q_hbm, y_hbm))
    targets = ((o_hbm, gq_hbm), (gk_hbm, gv_hbm))

    for phase in range(2):
        for c in range(chunks):
            cols = pl.ds(c * span, span)
            for a in range(2):
                pltpu.make_async_copy(
                    sources[phase][a].at[:, column(me, c)],
                    xin.at[2 * phase + a, strip(me), cols],
                    in_recv.at[phase, c],
                ).start()

    gains = pltpu.make_async_copy(gain_hbm, gain, gain_sem)
    gains.start()

    @pl.when(group == 0)
    def _():
        for c in range(chunks):
            pltpu.make_async_copy(
                s0_hbm.at[pl.ds(j * heads + c * step, step)],
                pin.at[pl.ds(c * step, step)],
                p_recv.at[c],
            ).start()

    if n_groups == 1:
        pl.semaphore_wait(barrier, peers - 1)
    else:
        inner = jnp.logical_and(group > 0, group < n_groups - 1)

        @pl.when(inner)
        def _():
            pl.semaphore_wait(barrier, peers + 1)

        @pl.when(jnp.logical_not(inner))
        def _():
            pl.semaphore_wait(barrier, peers)

    for phase in range(2):
        for c in range(chunks):
            cols = pl.ds(c * span, span)

            def scatter(p, carry, phase=phase, c=c, cols=cols):
                other, device = place(p)
                for a in range(2):
                    pltpu.make_async_remote_copy(
                        src_ref=sources[phase][a].at[:, column(other, c)],
                        dst_ref=xin.at[2 * phase + a, strip(me), cols],
                        send_sem=in_send.at[phase, c],
                        recv_sem=in_recv.at[phase, c],
                        device_id=device,
                        device_id_type=MESH,
                    ).start()
                return carry

            lax.fori_loop(1, peers, scatter, 0)

    def arrived(phase, c):
        ref = xin.at[pl.ds(2 * phase, 2), :, pl.ds(c * span, span)]
        pltpu.make_async_copy(ref, ref, in_recv.at[phase, c]).wait()

    def give(phase, c):
        cols = pl.ds(c * span, span)

        def back(p, carry):
            other, device = place(p)
            for a in range(2):
                pltpu.make_async_remote_copy(
                    src_ref=xout.at[2 * phase + a, strip(other), cols],
                    dst_ref=targets[phase][a].at[:, column(me, c)],
                    send_sem=out_send.at[phase, c],
                    recv_sem=out_recv.at[phase, c],
                    device_id=device,
                    device_id_type=MESH,
                ).start()
            return carry

        lax.fori_loop(1, peers, back, 0)
        for a in range(2):
            pltpu.make_async_copy(
                xout.at[2 * phase + a, strip(me), cols],
                targets[phase][a].at[:, column(me, c)],
                out_recv.at[phase, c],
            ).start()

    def state_copy(src, dst, send, recv, c, device):
        piece = pl.ds(c * step, step)
        return pltpu.make_async_remote_copy(
            src_ref=src.at[piece], dst_ref=dst.at[piece], send_sem=send.at[c],
            recv_sem=recv.at[c], device_id=device, device_id_type=MESH)

    def pass_prefix(c):
        piece = pl.ds(c * step, step)
        pltpu.make_async_copy(pin.at[piece], pin.at[piece], p_recv.at[c]).wait()

        @pl.when(group < n_groups - 1)
        def _():
            psend[c * step:(c + 1) * step] = (
                pin[c * step:(c + 1) * step] + tot[c * step:(c + 1) * step])
            state_copy(psend, pin, p_send, p_recv, c, later).start()

    for c in range(chunks):
        arrived(0, c)
        for h in range(c * step, (c + 1) * step):
            hc = slice(h * HEAD_DIM, (h + 1) * HEAD_DIM)
            run = jnp.zeros((HEAD_DIM, HEAD_DIM), F32)
            for b in range(sub):
                r = slice(b * block, (b + 1) * block)
                cum[h, b] = run
                run = run + dot(xin[0, r, hc], xin[1, r, hc], TN)
            tot[h] = run

        @pl.when(group == 0)
        def _(c=c):
            pass_prefix(c)

    row = lax.broadcasted_iota(jnp.int32, (block, block), 0)
    col = lax.broadcasted_iota(jnp.int32, (block, block), 1)
    causal = col <= row
    gains.wait()

    for c in range(chunks):
        @pl.when(group > 0)
        def _(c=c):
            pass_prefix(c)

    for c in range(chunks):
        arrived(1, c)
        for h in range(c * step, (c + 1) * step):
            hc = slice(h * HEAD_DIM, (h + 1) * HEAD_DIM)
            g = gain[pl.ds(j * heads + h, 1), :]
            carried = pin[h]
            run = jnp.zeros((HEAD_DIM, HEAD_DIM), F32)
            for b in reversed(range(sub)):
                r = slice(b * block, (b + 1) * block)
                k, v, q, up = xin[0, r, hc], xin[1, r, hc], xin[2, r, hc], xin[3, r, hc]
                state = (carried + cum[h, b]).astype(BF16)
                w = jnp.where(causal, dot(q, k, NT), 0.0).astype(BF16)
                att = dot(w, v, NN) + dot(q, state, NN)
                inv = lax.rsqrt(jnp.mean(att * att, axis=-1, keepdims=True) + EPSILON)
                normed = att * inv
                xout[0, r, hc] = (normed * g).astype(BF16)
                scaled = up.astype(F32) * g
                ga = ((scaled - normed * jnp.mean(scaled * normed, axis=-1, keepdims=True))
                      * inv).astype(BF16)
                gw = jnp.where(causal, dot(ga, v, NT), 0.0).astype(BF16)
                xout[1, r, hc] = (dot(gw, k, NN) + dot(ga, state, NT)).astype(BF16)
                part[0, r, hc] = dot(gw, q, TN)
                part[1, r, hc] = dot(w, ga, TN)
                gcum[h, b] = run
                run = run + dot(q, ga, TN)
            tot[h] = run

        @pl.when(jnp.logical_and(group == n_groups - 1, group > 0))
        def _(c=c):
            ssend[c * step:(c + 1) * step] = tot[c * step:(c + 1) * step]
            state_copy(ssend, sin, s_send, s_recv, c, earlier).start()

        give(0, c)

    for c in range(chunks):
        piece = pl.ds(c * step, step)

        @pl.when(group == n_groups - 1)
        def _(c=c):
            sin[c * step:(c + 1) * step] = jnp.zeros((step, HEAD_DIM, HEAD_DIM), F32)

        @pl.when(group < n_groups - 1)
        def _(c=c, piece=piece):
            pltpu.make_async_copy(sin.at[piece], sin.at[piece], s_recv.at[c]).wait()

            @pl.when(group > 0)
            def _():
                ssend[c * step:(c + 1) * step] = (
                    sin[c * step:(c + 1) * step] + tot[c * step:(c + 1) * step])
                state_copy(ssend, sin, s_send, s_recv, c, earlier).start()

        for h in range(c * step, (c + 1) * step):
            hc = slice(h * HEAD_DIM, (h + 1) * HEAD_DIM)
            after = sin[h]
            for b in range(sub):
                r = slice(b * block, (b + 1) * block)
                suffix = (after + gcum[h, b]).astype(BF16)
                xout[2, r, hc] = (part[0, r, hc] + dot(xin[1, r, hc], suffix, NT)).astype(BF16)
                xout[3, r, hc] = (part[1, r, hc] + dot(xin[0, r, hc], suffix, NN)).astype(BF16)
        give(1, c)

    for phase in range(2):
        for c in range(chunks):
            sent = xin.at[pl.ds(2 * phase, 2), pl.ds(0, (peers - 1) * rows), pl.ds(c * span, span)]
            pltpu.make_async_copy(sent, sent, in_send.at[phase, c]).wait()
            pltpu.make_async_copy(sent, sent, out_send.at[phase, c]).wait()
            whole = xout.at[pl.ds(2 * phase, 2), :, pl.ds(c * span, span)]
            pltpu.make_async_copy(whole, whole, out_recv.at[phase, c]).wait()
    for c in range(chunks):
        @pl.when(group < n_groups - 1)
        def _(c=c):
            state_copy(psend, pin, p_send, p_recv, c, later).wait_send()

        @pl.when(group > 0)
        def _(c=c):
            state_copy(ssend, sin, s_send, s_recv, c, earlier).wait_send()


def per_device(mesh, query, key, value, cotangent, gain, incoming_state):
    n_seq, n_head = mesh.shape["seq"], mesh.shape["head"]
    rows, features = query.shape
    local_heads = incoming_state.shape[0]
    sub = 1
    while sub < 4 and n_seq % (2 * sub) == 0 and local_heads % (2 * sub) == 0:
        sub *= 2
    heads = local_heads // sub
    step = max(1, heads // 4)
    chunks = heads // step
    tokens = rows * n_head * sub
    width = heads * HEAD_DIM
    plan = (n_seq // sub, sub, n_head, rows, heads, step)
    anywhere = pl.BlockSpec(memory_space=pl.ANY)
    resident = pl.BlockSpec(memory_space=pltpu.HBM)
    state = pltpu.VMEM((heads, HEAD_DIM, HEAD_DIM), F32)
    states = pltpu.VMEM((heads, sub, HEAD_DIM, HEAD_DIM), F32)
    sems = pltpu.SemaphoreType.DMA((2, chunks))
    chain = pltpu.SemaphoreType.DMA((chunks,))
    return pl.pallas_call(
        functools.partial(kernel, plan),
        out_shape=[jax.ShapeDtypeStruct((rows, features), BF16)] * 4,
        in_specs=[resident] * 6,
        out_specs=[anywhere] * 4,
        scratch_shapes=[
            pltpu.VMEM((4, tokens, width), BF16),
            pltpu.VMEM((4, tokens, width), BF16),
            pltpu.VMEM((2, tokens, width), F32),
            states, states, state, state, state, state, state,
            pltpu.VMEM((local_heads, HEAD_DIM), F32),
            sems, sems, sems, sems, chain, chain, chain, chain,
            pltpu.SemaphoreType.DMA,
        ],
        compiler_params=pltpu.CompilerParams(
            collective_id=0, has_side_effects=True, vmem_limit_bytes=48 * 1024 * 1024),
    )(query, key, value, cotangent, gain.reshape(local_heads, HEAD_DIM), incoming_state)


def solution(mesh):
    tokens = P(("seq", "head"), None)
    return jax.shard_map(
        functools.partial(per_device, mesh),
        mesh=mesh,
        in_specs=(tokens, tokens, tokens, tokens, P("head"), P("head", None, None)),
        out_specs=(tokens, tokens, tokens, tokens),
        check_vma=False,
    )
```

```python
import functools

import jax
import jax.numpy as jnp
from jax import lax
from jax.experimental import pallas as pl
from jax.experimental.pallas import tpu as pltpu
from jax.sharding import PartitionSpec as P

HEAD_DIM = 128
EPSILON = 1e-06
MESH = pl.DeviceIdType.MESH
F32 = jnp.float32
BF16 = jnp.bfloat16

NT = (((1,), (1,)), ((), ()))
TN = (((0,), (0,)), ((), ()))
NN = (((1,), (0,)), ((), ()))


def dot(a, b, dims):
    return lax.dot_general(a, b, dims, preferred_element_type=F32)


def kernel(plan, q_hbm, k_hbm, v_hbm, y_hbm, gain_hbm, s0_hbm, o_hbm, gq_hbm, gk_hbm, gv_hbm,
           xin, xout, part, cum, gcum, pin, psend, sin, ssend, tot, gain,
           in_send, in_recv, out_send, out_recv, p_send, p_recv, s_send, s_recv, gain_sem):
    n_groups, sub, n_head, rows, heads, step = plan
    peers = sub * n_head
    chunks = heads // step
    block = rows * n_head
    width = heads * HEAD_DIM
    span = step * HEAD_DIM
    seq, hd = lax.axis_index("seq"), lax.axis_index("head")
    group, j = seq // sub, lax.rem(seq, sub)
    me = j * n_head + hd

    def place(p):
        other = lax.rem(me + p, peers)
        return other, (group * sub + other // n_head, lax.rem(other, n_head))

    def column(other, c):
        owner = lax.rem(other, n_head) * (sub * heads) + (other // n_head) * heads + c * step
        return pl.ds(pl.multiple_of(owner * HEAD_DIM, span), span)

    def strip(index):
        return pl.ds(pl.multiple_of(index * rows, rows), rows)

    later = (seq + sub, hd)
    earlier = (seq - sub, hd)
    barrier = pltpu.get_barrier_semaphore()

    def greet(p, carry):
        _, device = place(p)
        pl.semaphore_signal(barrier, inc=1, device_id=device, device_id_type=MESH)
        return carry

    lax.fori_loop(1, peers, greet, 0)

    @pl.when(group > 0)
    def _():
        pl.semaphore_signal(barrier, inc=1, device_id=earlier, device_id_type=MESH)

    @pl.when(group < n_groups - 1)
    def _():
        pl.semaphore_signal(barrier, inc=1, device_id=later, device_id_type=MESH)

    sources = ((k_hbm, v_hbm), (q_hbm, y_hbm))
    targets = ((o_hbm, gq_hbm), (gk_hbm, gv_hbm))

    for phase in range(2):
        for c in range(chunks):
            cols = pl.ds(c * span, span)
            for a in range(2):
                pltpu.make_async_copy(
                    sources[phase][a].at[:, column(me, c)],
                    xin.at[2 * phase + a, strip(me), cols],
                    in_recv.at[phase, c],
                ).start()

    gains = pltpu.make_async_copy(gain_hbm, gain, gain_sem)
    gains.start()

    @pl.when(group == 0)
    def _():
        for c in range(chunks):
            pltpu.make_async_copy(
                s0_hbm.at[pl.ds(j * heads + c * step, step)],
                pin.at[pl.ds(c * step, step)],
                p_recv.at[c],
            ).start()

    if n_groups == 1:
        pl.semaphore_wait(barrier, peers - 1)
    else:
        inner = jnp.logical_and(group > 0, group < n_groups - 1)

        @pl.when(inner)
        def _():
            pl.semaphore_wait(barrier, peers + 1)

        @pl.when(jnp.logical_not(inner))
        def _():
            pl.semaphore_wait(barrier, peers)

    for phase in range(2):
        for c in range(chunks):
            cols = pl.ds(c * span, span)

            def scatter(p, carry, phase=phase, c=c, cols=cols):
                other, device = place(p)
                for a in range(2):
                    pltpu.make_async_remote_copy(
                        src_ref=sources[phase][a].at[:, column(other, c)],
                        dst_ref=xin.at[2 * phase + a, strip(me), cols],
                        send_sem=in_send.at[phase, c],
                        recv_sem=in_recv.at[phase, c],
                        device_id=device,
                        device_id_type=MESH,
                    ).start()
                return carry

            lax.fori_loop(1, peers, scatter, 0)

    def arrived(phase, c):
        ref = xin.at[pl.ds(2 * phase, 2), :, pl.ds(c * span, span)]
        pltpu.make_async_copy(ref, ref, in_recv.at[phase, c]).wait()

    def give(phase, c):
        cols = pl.ds(c * span, span)

        def back(p, carry):
            other, device = place(p)
            for a in range(2):
                pltpu.make_async_remote_copy(
                    src_ref=xout.at[2 * phase + a, strip(other), cols],
                    dst_ref=targets[phase][a].at[:, column(me, c)],
                    send_sem=out_send.at[phase, c],
                    recv_sem=out_recv.at[phase, c],
                    device_id=device,
                    device_id_type=MESH,
                ).start()
            return carry

        lax.fori_loop(1, peers, back, 0)
        for a in range(2):
            pltpu.make_async_copy(
                xout.at[2 * phase + a, strip(me), cols],
                targets[phase][a].at[:, column(me, c)],
                out_recv.at[phase, c],
            ).start()

    def state_copy(src, dst, send, recv, c, device):
        piece = pl.ds(c * step, step)
        return pltpu.make_async_remote_copy(
            src_ref=src.at[piece], dst_ref=dst.at[piece], send_sem=send.at[c],
            recv_sem=recv.at[c], device_id=device, device_id_type=MESH)

    def pass_prefix(c):
        piece = pl.ds(c * step, step)
        pltpu.make_async_copy(pin.at[piece], pin.at[piece], p_recv.at[c]).wait()

        @pl.when(group < n_groups - 1)
        def _():
            psend[c * step:(c + 1) * step] = (
                pin[c * step:(c + 1) * step] + tot[c * step:(c + 1) * step])
            state_copy(psend, pin, p_send, p_recv, c, later).start()

    for c in range(chunks):
        arrived(0, c)
        for h in range(c * step, (c + 1) * step):
            hc = slice(h * HEAD_DIM, (h + 1) * HEAD_DIM)
            run = jnp.zeros((HEAD_DIM, HEAD_DIM), F32)
            for b in range(sub):
                r = slice(b * block, (b + 1) * block)
                cum[h, b] = run
                run = run + dot(xin[0, r, hc], xin[1, r, hc], TN)
            tot[h] = run

        @pl.when(group == 0)
        def _(c=c):
            pass_prefix(c)

    row = lax.broadcasted_iota(jnp.int32, (block, block), 0)
    col = lax.broadcasted_iota(jnp.int32, (block, block), 1)
    causal = col <= row
    gains.wait()

    for c in range(chunks):
        @pl.when(group > 0)
        def _(c=c):
            pass_prefix(c)

    for c in range(chunks):
        arrived(1, c)
        for h in range(c * step, (c + 1) * step):
            hc = slice(h * HEAD_DIM, (h + 1) * HEAD_DIM)
            g = gain[pl.ds(j * heads + h, 1), :]
            carried = pin[h]
            run = jnp.zeros((HEAD_DIM, HEAD_DIM), F32)
            for b in reversed(range(sub)):
                r = slice(b * block, (b + 1) * block)
                k, v, q, up = xin[0, r, hc], xin[1, r, hc], xin[2, r, hc], xin[3, r, hc]
                state = (carried + cum[h, b]).astype(BF16)
                w = jnp.where(causal, dot(q, k, NT), 0.0).astype(BF16)
                att = dot(w, v, NN) + dot(q, state, NN)
                inv = lax.rsqrt(jnp.mean(att * att, axis=-1, keepdims=True) + EPSILON)
                normed = att * inv
                xout[0, r, hc] = (normed * g).astype(BF16)
                scaled = up.astype(F32) * g
                ga = ((scaled - normed * jnp.mean(scaled * normed, axis=-1, keepdims=True))
                      * inv).astype(BF16)
                gw = jnp.where(causal, dot(ga, v, NT), 0.0).astype(BF16)
                xout[1, r, hc] = (dot(gw, k, NN) + dot(ga, state, NT)).astype(BF16)
                part[0, r, hc] = dot(gw, q, TN)
                part[1, r, hc] = dot(w, ga, TN)
                gcum[h, b] = run
                run = run + dot(q, ga, TN)
            tot[h] = run

        @pl.when(jnp.logical_and(group == n_groups - 1, group > 0))
        def _(c=c):
            ssend[c * step:(c + 1) * step] = tot[c * step:(c + 1) * step]
            state_copy(ssend, sin, s_send, s_recv, c, earlier).start()

        give(0, c)

    for c in range(chunks):
        piece = pl.ds(c * step, step)

        @pl.when(group == n_groups - 1)
        def _(c=c):
            sin[c * step:(c + 1) * step] = jnp.zeros((step, HEAD_DIM, HEAD_DIM), F32)

        @pl.when(group < n_groups - 1)
        def _(c=c, piece=piece):
            pltpu.make_async_copy(sin.at[piece], sin.at[piece], s_recv.at[c]).wait()

            @pl.when(group > 0)
            def _():
                ssend[c * step:(c + 1) * step] = (
                    sin[c * step:(c + 1) * step] + tot[c * step:(c + 1) * step])
                state_copy(ssend, sin, s_send, s_recv, c, earlier).start()

        for h in range(c * step, (c + 1) * step):
            hc = slice(h * HEAD_DIM, (h + 1) * HEAD_DIM)
            after = sin[h]
            for b in range(sub):
                r = slice(b * block, (b + 1) * block)
                suffix = (after + gcum[h, b]).astype(BF16)
                xout[2, r, hc] = (part[0, r, hc] + dot(xin[1, r, hc], suffix, NT)).astype(BF16)
                xout[3, r, hc] = (part[1, r, hc] + dot(xin[0, r, hc], suffix, NN)).astype(BF16)
        give(1, c)

    for phase in range(2):
        for c in range(chunks):
            sent = xin.at[pl.ds(2 * phase, 2), pl.ds(0, (peers - 1) * rows), pl.ds(c * span, span)]
            pltpu.make_async_copy(sent, sent, in_send.at[phase, c]).wait()
            pltpu.make_async_copy(sent, sent, out_send.at[phase, c]).wait()
            whole = xout.at[pl.ds(2 * phase, 2), :, pl.ds(c * span, span)]
            pltpu.make_async_copy(whole, whole, out_recv.at[phase, c]).wait()
    for c in range(chunks):
        @pl.when(group < n_groups - 1)
        def _(c=c):
            state_copy(psend, pin, p_send, p_recv, c, later).wait_send()

        @pl.when(group > 0)
        def _(c=c):
            state_copy(ssend, sin, s_send, s_recv, c, earlier).wait_send()


def per_device(mesh, query, key, value, cotangent, gain, incoming_state):
    n_seq, n_head = mesh.shape["seq"], mesh.shape["head"]
    rows, features = query.shape
    local_heads = incoming_state.shape[0]
    sub = 1
    while sub < 4 and n_seq % (2 * sub) == 0 and local_heads % (2 * sub) == 0:
        sub *= 2
    heads = local_heads // sub
    step = max(1, heads // 4)
    chunks = heads // step
    tokens = rows * n_head * sub
    width = heads * HEAD_DIM
    plan = (n_seq // sub, sub, n_head, rows, heads, step)
    anywhere = pl.BlockSpec(memory_space=pl.ANY)
    resident = pl.BlockSpec(memory_space=pltpu.HBM)
    state = pltpu.VMEM((heads, HEAD_DIM, HEAD_DIM), F32)
    states = pltpu.VMEM((heads, sub, HEAD_DIM, HEAD_DIM), F32)
    sems = pltpu.SemaphoreType.DMA((2, chunks))
    chain = pltpu.SemaphoreType.DMA((chunks,))
    return pl.pallas_call(
        functools.partial(kernel, plan),
        out_shape=[jax.ShapeDtypeStruct((rows, features), BF16)] * 4,
        in_specs=[resident] * 6,
        out_specs=[anywhere] * 4,
        scratch_shapes=[
            pltpu.VMEM((4, tokens, width), BF16),
            pltpu.VMEM((4, tokens, width), BF16),
            pltpu.VMEM((2, tokens, width), F32),
            states, states, state, state, state, state, state,
            pltpu.VMEM((local_heads, HEAD_DIM), F32),
            sems, sems, sems, sems, chain, chain, chain, chain,
            pltpu.SemaphoreType.DMA,
        ],
        compiler_params=pltpu.CompilerParams(
            collective_id=0, has_side_effects=True, vmem_limit_bytes=51000 * 1024),
    )(query, key, value, cotangent, gain.reshape(local_heads, HEAD_DIM), incoming_state)


def solution(mesh):
    tokens = P(("seq", "head"), None)
    return jax.shard_map(
        functools.partial(per_device, mesh),
        mesh=mesh,
        in_specs=(tokens, tokens, tokens, tokens, P("head"), P("head", None, None)),
        out_specs=(tokens, tokens, tokens, tokens),
        check_vma=False,
    )
```
